512 devices in a mesh: leaf: 16 (over z), samp: 16 (over y, x), cblk: 2 (over core).
Axes of the slice: x: 4, y: 4, z: 16, core: 2. Of those that a mesh axis runs over, the one named last changes fastest.
Arguments:
- front_matrix: bfloat16 [32768, 32768], P('leaf', ('samp', 'cblk')), may hold values from -0.03125 to 0.03125
- pattern: int32 [32, 32], replicated, may hold values from 0 to 1, as said below
- sample: bfloat16 [256, 32768], P(None, ('samp', 'cblk')), may hold values from -6 to 6
- sketch: float32 [6, 256, 128], replicated, may hold values from -0.375 to 0.375
- level_ranks: int32 [6], replicated, may hold values from 96 to 128, as said below
Outputs:
- leaf_bases: float32 [128, 32768], P(None, ('leaf', 'cblk'))
- path_transfers: float32 [16, 5, 128, 256], P('leaf')
- root_sample: float32 [256, 256], P('samp')
The draws below stay inside these ranges and needn't reach their ends.
Inputs may be any that keep to these rules, and one draw needn't show every extreme that they name: pattern[a, a] is 1 for every a; other entries are 0 or 1. `level_ranks`: entry l is the rank kept at level l; entry 0 or entry 1 equals 128; entries past the tree's last level with a transfer are not read.
All inputs are finite; a program needn't handle non-finite values.
Results may differ from the reference program's by a relative error of at most 0.0033.
Values may be sent and summed in bfloat16 or wider, within the bound.
No kernel may reach another device: no remote copies, remote signals or barrier semaphores. Data moves between devices by JAX's collectives and lax.ppermute only.
A program may use at most 64 MiB of HBM per device.

```python
import jax
import jax.numpy as jnp
from jax import lax

LEAF_ROWS = 1024
SAMPLES = 256
RANK = 128
LEVELS = 6
MIN_RANK = 96
BLOCKS = 32
ORDER = 32768
N_LEAF = 16


def draw_pattern(key, part):
    coins = jax.random.randint(jax.random.fold_in(key, 11), (BLOCKS, BLOCKS), 0, 2)
    diagonal = jnp.arange(BLOCKS)[:, None] == jnp.arange(BLOCKS)[None, :]
    return jnp.where(diagonal, 1, coins).astype(jnp.int32)


def draw_level_ranks(key, part):
    values = jax.random.randint(jax.random.fold_in(key, 23), (LEVELS,), MIN_RANK, RANK + 1)
    chosen = jax.random.randint(jax.random.fold_in(key, 29), (), 0, 2)
    return jnp.where(jnp.arange(LEVELS) == chosen, RANK, values).astype(jnp.int32)


def shard_levels(rng, shape, pieces, smallest, top_value):
    def one(position, parts):
        heights = jax.random.uniform(jax.random.fold_in(jax.random.fold_in(rng, 6), position), (parts,), jnp.float32, smallest / len(pieces), top_value / len(pieces))
        return jnp.repeat(jnp.exp(heights), shape[position] // parts).reshape((-1,) + (1,) * (len(shape) - position - 1))

    factor_of = one(*pieces[0])
    for cut in pieces[1:]:
        factor_of = factor_of * one(*cut)
    return factor_of


def normal_values(own_key, shape, spread, limit, split=(), kind=jnp.bfloat16):
    array = spread * jax.random.normal(own_key, shape, jnp.float32)
    if split:
        array = array * shard_levels(own_key, shape, split, -0.22, 0.18)
    return jnp.clip(array, -limit, limit).astype(kind)


def setup_inputs(seed: int = 0) -> dict:
    keys = jax.random.split(jax.random.key(seed), 6)
    front_matrix = normal_values(keys[0], (ORDER, ORDER), ORDER ** -0.5, 0.03125, ((0, 16), (1, 32)))
    pattern = draw_pattern(jax.random.fold_in(keys[5], 71), 0)
    sample = normal_values(keys[2], (SAMPLES, ORDER), 1.0, 6.0, ((1, 32),))
    sketch = normal_values(keys[3], (LEVELS, SAMPLES, RANK), SAMPLES ** -0.5, 0.375, (), jnp.float32)
    level_ranks = draw_level_ranks(jax.random.fold_in(keys[5], 71), 0)
    return {"front_matrix": front_matrix, "pattern": pattern, "sample": sample, "sketch": sketch, "level_ranks": level_ranks}


def compress(columns, level_no, level_ranks, sketch):
    rank_top = sketch.shape[2]
    projected = jnp.einsum('nsm,sk->nkm', columns, sketch[level_no], precision=lax.Precision.HIGHEST)
    kept_mask = (jnp.arange(rank_top) < level_ranks[level_no]).astype(jnp.float32)
    projected = projected * kept_mask[:, None]
    gram_matrix = jnp.einsum('nkm,njm->nkj', projected, projected, precision=lax.Precision.HIGHEST) + jnp.diag(1.0 - kept_mask)
    factor = jnp.linalg.cholesky(gram_matrix)
    level_basis = jax.scipy.linalg.solve_triangular(factor, projected, lower=True)
    reduced = jnp.einsum('nsm,nkm->nsk', columns, level_basis, precision=lax.Precision.HIGHEST)
    return (level_basis, reduced)

def reference(front_matrix, pattern, sample, sketch, level_ranks):
    blocked = front_matrix.reshape(BLOCKS, LEAF_ROWS, BLOCKS, LEAF_ROWS)
    masked = (blocked * pattern.astype(jnp.bfloat16)[:, None, :, None]).reshape(ORDER, ORDER)
    contract_cols = (((1,), (1,)), ((), ()))
    first_sample = lax.dot_general(sample.astype(jnp.float32), masked.astype(jnp.float32), contract_cols, preferred_element_type=jnp.float32).astype(jnp.bfloat16)
    back_sample = jnp.dot(first_sample.astype(jnp.float32), masked.astype(jnp.float32), preferred_element_type=jnp.float32).astype(jnp.bfloat16)
    sampled = lax.dot_general(back_sample.astype(jnp.float32), masked.astype(jnp.float32), contract_cols, preferred_element_type=jnp.float32)
    columns = sampled.reshape(SAMPLES, BLOCKS, LEAF_ROWS).transpose(1, 0, 2)
    leaf_basis, reduced = compress(columns, 0, level_ranks, sketch)
    leaf_bases = leaf_basis.transpose(1, 0, 2).reshape(RANK, ORDER)
    tree_depth = N_LEAF.bit_length() - 1
    path_rows = []
    stacked = None
    for level_no in range(1, tree_depth + 2):
        stacked = jnp.concatenate([reduced[0::2], reduced[1::2]], axis=2)
        if level_no <= tree_depth:
            node_basis, reduced = compress(stacked, level_no, level_ranks, sketch)
            owner = (jnp.arange(N_LEAF) // 2 ** (level_no - 1)).astype(jnp.int32)
            path_rows.append(node_basis[owner])
    empty = jnp.zeros((N_LEAF, RANK, 2 * RANK), jnp.float32)
    path_rows = path_rows + [empty] * (LEVELS - 1 - len(path_rows))
    path_transfers = jnp.stack(path_rows, axis=1)
    root_sample = stacked[0]
    return (leaf_bases, path_transfers, root_sample)
```

```python
import jax
import jax.numpy as jnp
from jax import lax
from jax.experimental import pallas as pl
from jax.experimental.pallas import tpu as pltpu
from jax.sharding import PartitionSpec as P

HIGHEST = lax.Precision.HIGHEST
COLS = (((1,), (1,)), ((), ()))
ROWS = (((0,), (0,)), ((), ()))
ROW_BLOCK = 8


def exact_dot(a, b, dims):
    return lax.dot_general(a, b, dims, precision=HIGHEST, preferred_element_type=jnp.float32)


def inverse_factor(gram):
    n = gram.shape[0]
    count = n // ROW_BLOCK
    lane = lax.broadcasted_iota(jnp.int32, (ROW_BLOCK, n), 1)
    row = lax.broadcasted_iota(jnp.int32, (ROW_BLOCK, n), 0)
    panels = [gram[ROW_BLOCK * i : ROW_BLOCK * (i + 1), :] for i in range(count)]
    finished = []
    for b in range(count):
        panel = panels[b]
        start = ROW_BLOCK * b
        stop = start + ROW_BLOCK
        columns = [
            jnp.broadcast_to(panel[:, start + j : start + j + 1], (ROW_BLOCK, n))
            for j in range(ROW_BLOCK)
        ]
        root = jnp.zeros((ROW_BLOCK, n), jnp.float32)
        inverse = jnp.zeros((ROW_BLOCK, n), jnp.float32)
        for k in range(ROW_BLOCK):
            pivot = jnp.broadcast_to(columns[k][k : k + 1, :], (ROW_BLOCK, n))
            over = 1.0 / pivot
            factor = jnp.where(row > k, columns[k] * over, 0.0)
            here = lane == start + k
            pivot_row = jnp.where(here, 1.0, jnp.broadcast_to(panel[k : k + 1, :], (ROW_BLOCK, n)))
            panel = jnp.where(here & (row >= k), jnp.where(row == k, 1.0, 0.0), panel)
            panel = panel - factor * pivot_row
            for j in range(k + 1, ROW_BLOCK):
                columns[j] = columns[j] - factor * jnp.broadcast_to(
                    columns[j][k : k + 1, :], (ROW_BLOCK, n)
                )
            inverse = jnp.where(row == k, over, inverse)
            root = jnp.where(row == k, lax.rsqrt(pivot), root)
        panel = jnp.where((lane <= start + row) | (lane >= stop), panel, 0.0)
        finished.append(panel * jnp.where(lane < stop, root, 0.0))
        if b + 1 < count:
            scaled = panel * inverse
            outside = (lane < start) | (lane >= stop)
            update = exact_dot(scaled[:, stop : stop + ROW_BLOCK], panel, ROWS)
            panels[b + 1] = jnp.where(outside, panels[b + 1], 0.0) - update
            if b + 2 < count:
                update = exact_dot(scaled[:, stop + ROW_BLOCK :], panel, ROWS)
                for i in range(b + 2, count):
                    at = ROW_BLOCK * (i - b - 2)
                    panels[i] = jnp.where(outside, panels[i], 0.0) - update[at : at + ROW_BLOCK, :]
    return jnp.concatenate(finished, axis=0)


def compress_values(parts, weights, rank):
    top = weights.shape[1]
    keep = (lax.broadcasted_iota(jnp.int32, (top, 1), 0) < rank).astype(jnp.float32)
    views = [exact_dot(weights, part, ROWS) * keep for part in parts]
    gram = sum(exact_dot(view, view, COLS) for view in views)
    at_row = lax.broadcasted_iota(jnp.int32, (top, top), 0)
    at_col = lax.broadcasted_iota(jnp.int32, (top, top), 1)
    gram = gram + jnp.where((at_row == at_col) & (at_row >= rank), 1.0, 0.0)
    cross = sum(exact_dot(part, view, COLS) for part, view in zip(parts, views, strict=True))
    inverse = inverse_factor(gram)
    bases = [exact_dot(inverse, view, (((1,), (0,)), ((), ()))) for view in views]
    return bases, exact_dot(cross, inverse, COLS)


def leaf_kernel(rank_ref, columns_ref, weights_ref, basis_ref, reduced_ref):
    bases, reduced = compress_values([columns_ref[...]], weights_ref[...], rank_ref[0])
    basis_ref[...] = bases[0]
    reduced_ref[...] = reduced


def node_kernel(rank_ref, mine_ref, other_ref, weights_ref, basis_ref, reduced_ref):
    upper = rank_ref[1] == 1
    mine = mine_ref[...]
    other = other_ref[...]
    parts = [jnp.where(upper, other, mine), jnp.where(upper, mine, other)]
    bases, reduced = compress_values(parts, weights_ref[...], rank_ref[0])
    top = weights_ref.shape[1]
    basis_ref[:, :top] = bases[0]
    basis_ref[:, top:] = bases[1]
    reduced_ref[...] = reduced


def compress(scalars, parts, weights):
    samples, top = weights.shape
    width = sum(part.shape[1] for part in parts)
    kernel = leaf_kernel if len(parts) == 1 else node_kernel
    vmem = pl.BlockSpec(memory_space=pltpu.VMEM)
    return pl.pallas_call(
        kernel,
        in_specs=[pl.BlockSpec(memory_space=pltpu.SMEM)] + [vmem] * (len(parts) + 1),
        out_specs=(vmem, vmem),
        out_shape=(
            jax.ShapeDtypeStruct((top, width), jnp.float32),
            jax.ShapeDtypeStruct((samples, top), jnp.float32),
        ),
        name="compress_leaf" if len(parts) == 1 else "compress_node",
    )(scalars, *parts, weights)


def swap_cores(x):
    return lax.ppermute(x, "cblk", [(0, 1), (1, 0)])


def exchange(x, axis, groups=None):
    return lax.all_to_all(x, axis, 0, 0, axis_index_groups=groups)


def spread(x, count, axis, groups=None):
    return exchange(jnp.broadcast_to(x[None], (count,) + x.shape), axis, groups)


def body(front, pattern, sample, sketch, level_ranks):
    rows, width = front.shape
    leaf_rows = rows // 2
    samples = sample.shape[0]
    half = samples // 2
    top = sketch.shape[2]
    n_leaf = lax.axis_size("leaf")
    n_samp = lax.axis_size("samp")
    depth = n_leaf.bit_length() - 1
    z = lax.axis_index("leaf")
    s = lax.axis_index("samp")
    c = lax.axis_index("cblk")
    f32 = jnp.float32
    bf16 = jnp.bfloat16

    block = 2 * s + c
    flags = lax.dynamic_slice(pattern, (2 * z, block), (2, 1))
    leaf_mask = jnp.repeat(flags, leaf_rows, axis=0).reshape(1, rows)

    def first_half(which):
        part = lax.dynamic_slice_in_dim(sample, which * half, half, 0)
        return lax.dot_general(part, front, COLS, preferred_element_type=f32)

    away = swap_cores(first_half(1 - c) * leaf_mask.astype(f32))
    total = first_half(c) * leaf_mask.astype(f32) + away
    pieces = exchange(total.reshape(n_samp, half // n_samp, rows), "samp")
    piece = jnp.sum(pieces, axis=0).astype(bf16)
    mine = spread(piece, n_samp, "samp").reshape(half, rows)
    other = swap_cores(mine)
    first_sample = jnp.where(
        c == 0, jnp.concatenate([mine, other], 0), jnp.concatenate([other, mine], 0)
    )
    first_sample = first_sample * leaf_mask.astype(bf16)

    back_part = jnp.dot(first_sample, front, preferred_element_type=f32)
    odd = z % 2
    pairs = []
    for i in range(n_leaf):
        pairs.append((2 * i, 2 * (i ^ 1)))
        pairs.append((2 * i + 1, 2 * ((i + 1 if i % 2 else i - 1) % n_leaf) + 1))
    group = n_leaf // 2
    parity = [list(range(p, n_leaf, 2)) for p in range(2)]
    given = lax.dynamic_slice_in_dim(back_part, (1 - odd) * half, half, 0)
    kept = lax.dynamic_slice_in_dim(back_part, odd * half, half, 0)
    kept = kept + lax.ppermute(given, ("leaf", "cblk"), pairs)
    pieces = exchange(kept.reshape(group, half // group, width), "leaf", parity)
    piece = jnp.sum(pieces, axis=0).astype(bf16)
    mine = spread(piece, group, "leaf", parity).reshape(half, width)
    other = lax.ppermute(mine, ("leaf", "cblk"), pairs)
    back_sample = jnp.where(
        odd == 0, jnp.concatenate([mine, other], 0), jnp.concatenate([other, mine], 0)
    )

    def third_half(which):
        part = lax.dynamic_slice_in_dim(front, which * leaf_rows, leaf_rows, 0)
        flag = lax.dynamic_slice_in_dim(flags, which, 1, 0).astype(f32)
        return lax.dot_general(back_sample, part, COLS, preferred_element_type=f32) * flag

    away = swap_cores(third_half(1 - c))
    total = third_half(c) + away
    pieces = exchange(total.reshape(n_samp, samples // n_samp, leaf_rows), "samp")
    piece = jnp.sum(pieces, axis=0)
    leaf_columns = spread(piece, n_samp, "samp").reshape(samples, leaf_rows)

    def scalars(level, upper):
        return jnp.stack([level_ranks[level], upper.astype(jnp.int32)])

    leaf_basis, reduced = compress(scalars(0, c), [leaf_columns], sketch[0])
    path = []
    node_basis, reduced = compress(scalars(1, c), [reduced, swap_cores(reduced)], sketch[1])
    path.append(node_basis)
    for bit in range(depth - 1):
        partner = lax.ppermute(reduced, "leaf", [(i, i ^ (1 << bit)) for i in range(n_leaf)])
        node_basis, reduced = compress(
            scalars(bit + 2, z // 2**bit % 2), [reduced, partner], sketch[bit + 2]
        )
        path.append(node_basis)
    share = samples // n_samp
    mine = lax.dynamic_slice_in_dim(reduced, s * share, share, 0)
    bit = depth - 1
    other = lax.ppermute(mine, "leaf", [(i, i ^ (1 << bit)) for i in range(n_leaf)])
    upper = z // 2**bit % 2 == 1
    root = jnp.concatenate([jnp.where(upper, other, mine), jnp.where(upper, mine, other)], axis=1)
    empty = jnp.zeros((top, 2 * top), f32)
    path = path + [empty] * (sketch.shape[0] - 1 - len(path))
    return (leaf_basis, jnp.stack(path)[None], root)


def solution(mesh):
    placed = (P("leaf", ("samp", "cblk")), P(), P(None, ("samp", "cblk")), P(), P())
    return jax.shard_map(
        body,
        mesh=mesh,
        in_specs=placed,
        out_specs=(P(None, ("leaf", "cblk")), P("leaf", None, None, None), P("samp", None)),
        check_vma=False,
    )
```

```python
import functools

import jax
import jax.numpy as jnp
from jax import lax
from jax.experimental import pallas as pl
from jax.experimental.pallas import tpu as pltpu
from jax.sharding import PartitionSpec as P

HIGHEST = lax.Precision.HIGHEST
COLS = (((1,), (1,)), ((), ()))
ROWS = (((0,), (0,)), ((), ()))
ROW_BLOCK = 16
LANES = 128
VMEM_LIMIT = 16 << 20


def exact_dot(a, b, dims):
    return lax.dot_general(a, b, dims, precision=HIGHEST, preferred_element_type=jnp.float32)


def inverse_factor(gram):
    n = gram.shape[0]
    count = n // ROW_BLOCK
    lane = lax.broadcasted_iota(jnp.int32, (ROW_BLOCK, n), 1)
    row = lax.broadcasted_iota(jnp.int32, (ROW_BLOCK, n), 0)
    panels = [gram[ROW_BLOCK * i : ROW_BLOCK * (i + 1), :] for i in range(count)]
    finished = []
    for b in range(count):
        panel = panels[b]
        start = ROW_BLOCK * b
        stop = start + ROW_BLOCK
        columns = [
            jnp.broadcast_to(panel[:, start + j : start + j + 1], (ROW_BLOCK, n))
            for j in range(ROW_BLOCK)
        ]
        root = jnp.zeros((ROW_BLOCK, n), jnp.float32)
        inverse = jnp.zeros((ROW_BLOCK, n), jnp.float32)
        for k in range(ROW_BLOCK):
            pivot = jnp.broadcast_to(columns[k][k : k + 1, :], (ROW_BLOCK, n))
            over = 1.0 / pivot
            factor = jnp.where(row > k, columns[k] * over, 0.0)
            here = lane == start + k
            pivot_row = jnp.where(here, 1.0, jnp.broadcast_to(panel[k : k + 1, :], (ROW_BLOCK, n)))
            panel = jnp.where(here & (row >= k), jnp.where(row == k, 1.0, 0.0), panel)
            panel = panel - factor * pivot_row
            for j in range(k + 1, ROW_BLOCK):
                columns[j] = columns[j] - factor * jnp.broadcast_to(
                    columns[j][k : k + 1, :], (ROW_BLOCK, n)
                )
            inverse = jnp.where(row == k, over, inverse)
            root = jnp.where(row == k, lax.rsqrt(pivot), root)
        panel = jnp.where((lane <= start + row) | (lane >= stop), panel, 0.0)
        finished.append(panel * jnp.where(lane < stop, root, 0.0))
        if b + 1 < count:
            scaled = panel * inverse
            outside = (lane < start) | (lane >= stop)
            update = exact_dot(scaled[:, stop:], panel, ROWS)
            for i in range(b + 1, count):
                at = ROW_BLOCK * (i - b - 1)
                panels[i] = jnp.where(outside, panels[i], 0.0) - update[at : at + ROW_BLOCK, :]
    return jnp.concatenate(finished, axis=0)


def compress_values(parts, weights, rank):
    top = weights.shape[1]
    keep = (lax.broadcasted_iota(jnp.int32, (top, 1), 0) < rank).astype(jnp.float32)
    views = [exact_dot(weights, part, ROWS) * keep for part in parts]
    gram = sum(exact_dot(view, view, COLS) for view in views)
    at_row = lax.broadcasted_iota(jnp.int32, (top, top), 0)
    at_col = lax.broadcasted_iota(jnp.int32, (top, top), 1)
    gram = gram + jnp.where((at_row == at_col) & (at_row >= rank), 1.0, 0.0)
    cross = sum(exact_dot(part, view, COLS) for part, view in zip(parts, views, strict=True))
    inverse = inverse_factor(gram)
    bases = [exact_dot(inverse, view, (((1,), (0,)), ((), ()))) for view in views]
    return bases, exact_dot(cross, inverse, COLS)


def leaf_kernel(level, table_ref, columns_ref, weights_ref, basis_ref, reduced_ref):
    rank = table_ref[level, 0]
    columns = jnp.concatenate([decode(columns_ref[i]) for i in range(columns_ref.shape[0])], axis=0)
    bases, reduced = compress_values([columns], weights_ref[...], rank)
    basis_ref[...] = bases[0]
    reduced_ref[...] = reduced


def node_kernel(level, table_ref, mine_ref, other_ref, weights_ref, basis_ref, reduced_ref):
    upper = table_ref[level, 1] == 1
    mine = mine_ref[...]
    other = other_ref[...]
    parts = [jnp.where(upper, other, mine), jnp.where(upper, mine, other)]
    bases, reduced = compress_values(parts, weights_ref[...], table_ref[level, 0])
    top = weights_ref.shape[1]
    basis_ref[:, :top] = bases[0]
    basis_ref[:, top:] = bases[1]
    reduced_ref[...] = reduced


def compress(level, table, parts, weights):
    samples, top = weights.shape
    width = parts[0].shape[-1] - LANES if len(parts) == 1 else 2 * top
    kernel = leaf_kernel if len(parts) == 1 else node_kernel
    vmem = pl.BlockSpec(memory_space=pltpu.VMEM)
    return pl.pallas_call(
        functools.partial(kernel, level),
        in_specs=[pl.BlockSpec(memory_space=pltpu.SMEM)] + [vmem] * (len(parts) + 1),
        out_specs=(vmem, vmem),
        out_shape=(
            jax.ShapeDtypeStruct((top, width), jnp.float32),
            jax.ShapeDtypeStruct((samples, top), jnp.float32),
        ),
        compiler_params=pltpu.CompilerParams(vmem_limit_bytes=VMEM_LIMIT),
        name="compress_leaf" if len(parts) == 1 else "compress_node",
    )(table, *parts, weights)


def swap_cores(x):
    return lax.ppermute(x, "cblk", [(0, 1), (1, 0)])


def exchange(x, axis):
    return lax.all_to_all(x, axis, 0, 0)


def encode(x):
    lane = lax.broadcasted_iota(jnp.int32, (x.shape[0], LANES), 1)
    tail = jnp.zeros((x.shape[0], LANES), jnp.float32)
    tiles = []
    for g in range(x.shape[1] // LANES):
        tile = x[:, g * LANES : (g + 1) * LANES]
        top = jnp.max(jnp.abs(tile), axis=1, keepdims=True)
        bits = jnp.clip(14.0 - jnp.ceil(jnp.log2(top)), -120.0, 120.0)
        bits = jnp.broadcast_to(jnp.where(top > 0, bits, 0.0), tile.shape)
        tiles.append(jnp.round(tile * jnp.exp2(bits)))
        tail = jnp.where(lane == g, bits, tail)
    return jnp.concatenate(tiles + [tail], axis=1).astype(jnp.int32).astype(jnp.int16)


def decode(message):
    wide = message.astype(jnp.int32).astype(jnp.float32)
    width = wide.shape[1] - LANES
    scale = jnp.exp2(-wide[:, width:])
    return jnp.concatenate(
        [
            wide[:, g * LANES : (g + 1) * LANES] * scale[:, g : g + 1]
            for g in range(width // LANES)
        ],
        axis=1,
    )


def encode_kernel(*refs):
    out_ref = refs[-1]
    count, rows, _ = out_ref.shape
    for i in range(count):
        at = pl.ds(i * rows, rows)
        out_ref[i] = encode(sum(ref[at, :] for ref in refs[:-1]))


def merge_kernel(message_ref, out_ref):
    total = decode(message_ref[0])
    for i in range(1, message_ref.shape[0]):
        total = total + decode(message_ref[i])
    if out_ref.dtype == jnp.int16:
        value = encode(total)
    else:
        value = total.astype(out_ref.dtype)
    for i in range(out_ref.shape[0]):
        out_ref[i] = value


def packed(parts, count):
    rows, width = parts[0].shape
    out = jax.ShapeDtypeStruct((count, rows // count, width + LANES), jnp.int16)
    return whole_call(encode_kernel, parts, out, "encode")


def merged(message, dtype):
    count, rows, width = message.shape
    width = width if dtype == jnp.int16 else width - LANES
    out = jax.ShapeDtypeStruct((count, rows, width), dtype)
    return whole_call(merge_kernel, [message], out, "merge")


def whole_call(kernel, operands, out, name):
    vmem = pl.BlockSpec(memory_space=pltpu.VMEM)
    return pl.pallas_call(
        kernel,
        in_specs=[vmem] * len(operands),
        out_specs=vmem,
        out_shape=out,
        compiler_params=pltpu.CompilerParams(vmem_limit_bytes=VMEM_LIMIT),
        name=name,
    )(*operands)


def body(front, pattern, sample, sketch, level_ranks):
    rows, width = front.shape
    leaf_rows = rows // 2
    samples = sample.shape[0]
    half = samples // 2
    top = sketch.shape[2]
    n_leaf = lax.axis_size("leaf")
    n_samp = lax.axis_size("samp")
    depth = n_leaf.bit_length() - 1
    z = lax.axis_index("leaf")
    s = lax.axis_index("samp")
    c = lax.axis_index("cblk")
    f32 = jnp.float32
    bf16 = jnp.bfloat16

    block = 2 * s + c
    flags = lax.dynamic_slice(pattern, (2 * z, block), (2, 1))
    leaf_mask = jnp.repeat(flags, leaf_rows, axis=0).reshape(1, rows)

    def first_half(which):
        part = lax.dynamic_slice_in_dim(sample, which * half, half, 0)
        return lax.dot_general(part, front, COLS, preferred_element_type=f32)

    away = swap_cores(first_half(1 - c) * leaf_mask.astype(f32))
    message = packed([first_half(c) * leaf_mask.astype(f32), away], n_samp)
    pieces = merged(exchange(message, "samp"), bf16)
    mine = exchange(pieces, "samp").reshape(half, rows)
    other = swap_cores(mine)
    first_sample = jnp.where(
        c == 0, jnp.concatenate([mine, other], 0), jnp.concatenate([other, mine], 0)
    )
    first_sample = first_sample * leaf_mask.astype(bf16)

    back_part = jnp.dot(first_sample, front, preferred_element_type=f32)
    pieces = merged(exchange(packed([back_part], n_leaf), "leaf"), bf16)
    back_sample = exchange(pieces, "leaf").reshape(samples, width)

    def third_half(which):
        part = lax.dynamic_slice_in_dim(front, which * leaf_rows, leaf_rows, 0)
        flag = lax.dynamic_slice_in_dim(flags, which, 1, 0).astype(f32)
        return lax.dot_general(back_sample, part, COLS, preferred_element_type=f32) * flag

    away = swap_cores(third_half(1 - c))
    message = packed([third_half(c), away], n_samp)
    columns = exchange(merged(exchange(message, "samp"), jnp.int16), "samp")

    uppers = [c, c] + [z // 2**bit % 2 for bit in range(depth - 1)]
    table = jnp.stack([level_ranks[: len(uppers)], jnp.stack(uppers).astype(jnp.int32)], axis=1)
    leaf_basis, reduced = compress(0, table, [columns], sketch[0])
    path = []
    node_basis, reduced = compress(1, table, [reduced, swap_cores(reduced)], sketch[1])
    path.append(node_basis)
    for bit in range(depth - 1):
        partner = lax.ppermute(reduced, "leaf", [(i, i ^ (1 << bit)) for i in range(n_leaf)])
        node_basis, reduced = compress(bit + 2, table, [reduced, partner], sketch[bit + 2])
        path.append(node_basis)
    share = samples // n_samp
    mine = lax.dynamic_slice_in_dim(reduced, s * share, share, 0)
    bit = depth - 1
    other = lax.ppermute(mine, "leaf", [(i, i ^ (1 << bit)) for i in range(n_leaf)])
    upper = z // 2**bit % 2 == 1
    root = jnp.concatenate([jnp.where(upper, other, mine), jnp.where(upper, mine, other)], axis=1)
    empty = jnp.zeros((top, 2 * top), f32)
    path = path + [empty] * (sketch.shape[0] - 1 - len(path))
    return (leaf_basis, jnp.stack(path)[None], root)


def solution(mesh):
    placed = (P("leaf", ("samp", "cblk")), P(), P(None, ("samp", "cblk")), P(), P())
    return jax.shard_map(
        body,
        mesh=mesh,
        in_specs=placed,
        out_specs=(P(None, ("leaf", "cblk")), P("leaf", None, None, None), P("samp", None)),
        check_vma=False,
    )
```

```python
import functools

import jax
import jax.numpy as jnp
from jax import lax
from jax.experimental import pallas as pl
from jax.experimental.pallas import tpu as pltpu
from jax.sharding import PartitionSpec as P

HIGHEST = lax.Precision.HIGHEST
COLS = (((1,), (1,)), ((), ()))
ROWS = (((0,), (0,)), ((), ()))
ROW_BLOCK = 16
LANES = 128
FOLD = 8
TILE = 8
VMEM_LIMIT = 16 << 20


def exact_dot(a, b, dims):
    return lax.dot_general(a, b, dims, precision=HIGHEST, preferred_element_type=jnp.float32)


def inverse_factor(gram):
    n = gram.shape[0]
    count = n // ROW_BLOCK
    lane = lax.broadcasted_iota(jnp.int32, (ROW_BLOCK, n), 1)
    row = lax.broadcasted_iota(jnp.int32, (ROW_BLOCK, n), 0)
    panels = [gram[ROW_BLOCK * i : ROW_BLOCK * (i + 1), :] for i in range(count)]
    finished = []
    for b in range(count):
        panel = panels[b]
        start = ROW_BLOCK * b
        stop = start + ROW_BLOCK
        columns = [
            jnp.broadcast_to(panel[:, start + j : start + j + 1], (ROW_BLOCK, n))
            for j in range(ROW_BLOCK)
        ]
        root = jnp.zeros((ROW_BLOCK, n), jnp.float32)
        inverse = jnp.zeros((ROW_BLOCK, n), jnp.float32)
        for k in range(ROW_BLOCK):
            pivot = jnp.broadcast_to(columns[k][k : k + 1, :], (ROW_BLOCK, n))
            over = 1.0 / pivot
            factor = jnp.where(row > k, columns[k] * over, 0.0)
            here = lane == start + k
            pivot_row = jnp.where(here, 1.0, jnp.broadcast_to(panel[k : k + 1, :], (ROW_BLOCK, n)))
            panel = jnp.where(here & (row >= k), jnp.where(row == k, 1.0, 0.0), panel)
            panel = panel - factor * pivot_row
            for j in range(k + 1, ROW_BLOCK):
                columns[j] = columns[j] - factor * jnp.broadcast_to(
                    columns[j][k : k + 1, :], (ROW_BLOCK, n)
                )
            inverse = jnp.where(row == k, over, inverse)
            root = jnp.where(row == k, lax.rsqrt(pivot), root)
        panel = jnp.where((lane <= start + row) | (lane >= stop), panel, 0.0)
        finished.append(panel * jnp.where(lane < stop, root, 0.0))
        if b + 1 < count:
            scaled = panel * inverse
            outside = (lane < start) | (lane >= stop)
            update = exact_dot(scaled[:, stop:], panel, ROWS)
            for i in range(b + 1, count):
                at = ROW_BLOCK * (i - b - 1)
                panels[i] = jnp.where(outside, panels[i], 0.0) - update[at : at + ROW_BLOCK, :]
    return jnp.concatenate(finished, axis=0)


def compress_values(parts, weights, rank):
    top = weights.shape[1]
    keep = (lax.broadcasted_iota(jnp.int32, (top, 1), 0) < rank).astype(jnp.float32)
    views = [exact_dot(weights, part, ROWS) * keep for part in parts]
    gram = sum(exact_dot(view, view, COLS) for view in views)
    at_row = lax.broadcasted_iota(jnp.int32, (top, top), 0)
    at_col = lax.broadcasted_iota(jnp.int32, (top, top), 1)
    gram = gram + jnp.where((at_row == at_col) & (at_row >= rank), 1.0, 0.0)
    cross = sum(exact_dot(part, view, COLS) for part, view in zip(parts, views, strict=True))
    inverse = inverse_factor(gram)
    bases = [exact_dot(inverse, view, (((1,), (0,)), ((), ()))) for view in views]
    return bases, exact_dot(cross, inverse, COLS)


def fold(x):
    rows = x.shape[0] // FOLD
    return jnp.concatenate([x[i * rows : (i + 1) * rows, :] for i in range(FOLD)], axis=1)


def unfold(x):
    width = x.shape[1] // FOLD
    return jnp.concatenate([x[:, i * width : (i + 1) * width] for i in range(FOLD)], axis=0)


def leaf_kernel(level, table_ref, columns_ref, weights_ref, basis_ref, reduced_ref, message_ref):
    rank = table_ref[level, 0]
    share = weights_ref.shape[0] // columns_ref.shape[0]
    columns = jnp.concatenate(
        [stacked_rows(decode(columns_ref[i]), share) for i in range(columns_ref.shape[0])], axis=0
    )
    bases, reduced = compress_values([columns], weights_ref[...], rank)
    basis_ref[...] = bases[0]
    reduced_ref[...] = reduced
    message_ref[...] = encode(fold(reduced))


def node_kernel(
    level, table_ref, mine_ref, other_ref, weights_ref, basis_ref, reduced_ref, message_ref=None
):
    upper = table_ref[level, 1] == 1
    mine = mine_ref[...]
    other = unfold(decode(other_ref[...]))
    parts = [jnp.where(upper, other, mine), jnp.where(upper, mine, other)]
    bases, reduced = compress_values(parts, weights_ref[...], table_ref[level, 0])
    top = weights_ref.shape[1]
    basis_ref[:, :top] = bases[0]
    basis_ref[:, top:] = bases[1]
    reduced_ref[...] = reduced
    if message_ref is not None:
        message_ref[...] = encode(fold(reduced))


def compress(level, table, parts, weights, last=False):
    samples, top = weights.shape
    width = (parts[0].shape[-1] - LANES) * parts[0].shape[0] * TILE // samples if len(parts) == 1 else 2 * top
    kernel = leaf_kernel if len(parts) == 1 else node_kernel
    vmem = pl.BlockSpec(memory_space=pltpu.VMEM)
    outs = [
        jax.ShapeDtypeStruct((top, width), jnp.float32),
        jax.ShapeDtypeStruct((samples, top), jnp.float32),
        jax.ShapeDtypeStruct((samples // FOLD, FOLD * top + LANES), jnp.int16),
    ]
    outs = outs[:2] if last else outs
    return pl.pallas_call(
        functools.partial(kernel, level),
        in_specs=[pl.BlockSpec(memory_space=pltpu.SMEM)] + [vmem] * (len(parts) + 1),
        out_specs=(vmem,) * len(outs),
        out_shape=tuple(outs),
        compiler_params=pltpu.CompilerParams(vmem_limit_bytes=VMEM_LIMIT),
        name="compress_leaf" if len(parts) == 1 else "compress_node",
    )(table, *parts, weights)


def swap_cores(x):
    return lax.ppermute(x, "cblk", [(0, 1), (1, 0)])


def exchange(x, axis, groups=None):
    return lax.all_to_all(x, axis, 0, 0, axis_index_groups=groups)


def encode(x):
    lane = lax.broadcasted_iota(jnp.int32, (x.shape[0], LANES), 1)
    tail = jnp.zeros((x.shape[0], LANES), jnp.float32)
    tiles = []
    for g in range(x.shape[1] // LANES):
        tile = x[:, g * LANES : (g + 1) * LANES]
        top = jnp.max(jnp.abs(tile), axis=1, keepdims=True)
        bits = jnp.clip(15.0 - jnp.ceil(jnp.log2(top * 1.001)), -120.0, 120.0)
        bits = jnp.broadcast_to(jnp.where(top > 0, bits, 0.0), tile.shape)
        tiles.append(jnp.round(tile * jnp.exp2(bits)))
        tail = jnp.where(lane == g, bits, tail)
    return jnp.concatenate(tiles + [tail], axis=1).astype(jnp.int32).astype(jnp.int16)


def decode(message):
    wide = message.astype(jnp.int32).astype(jnp.float32)
    width = wide.shape[1] - LANES
    scale = jnp.exp2(-wide[:, width:])
    return jnp.concatenate(
        [
            wide[:, g * LANES : (g + 1) * LANES] * scale[:, g : g + 1]
            for g in range(width // LANES)
        ],
        axis=1,
    )


def side_by_side(x):
    return jnp.concatenate([x[:TILE, :], x[TILE:, :]], axis=1) if x.shape[0] > TILE else x


def stacked_rows(x, rows):
    if rows == TILE:
        return x
    width = x.shape[1] // 2
    return jnp.concatenate([x[:, :width], x[:, width:]], axis=0)


def encode_kernel(*refs):
    out_ref = refs[-1]
    count = out_ref.shape[0]
    rows = refs[0].shape[0] // count
    for i in range(count):
        at = pl.ds(i * rows, rows)
        out_ref[i] = encode(side_by_side(sum(ref[at, :] for ref in refs[:-1])))


def give_kernel(parity_ref, part_ref, out_ref):
    count = out_ref.shape[0]
    rows = part_ref.shape[0] // (2 * count)
    other = 1 - parity_ref[0]
    for i in range(count):
        at = pl.multiple_of((2 * i + other) * rows, rows)
        out_ref[i] = encode(side_by_side(part_ref[pl.ds(at, rows), :]))


def keep_kernel(parity_ref, part_ref, message_ref, out_ref):
    count = out_ref.shape[0]
    rows = part_ref.shape[0] // (2 * count)
    for i in range(count):
        at = pl.multiple_of((2 * i + parity_ref[0]) * rows, rows)
        kept = side_by_side(part_ref[pl.ds(at, rows), :])
        out_ref[i] = encode(kept + decode(message_ref[i]))


def merge_kernel(message_ref, out_ref):
    total = decode(message_ref[0])
    for i in range(1, message_ref.shape[0]):
        total = total + decode(message_ref[i])
    if out_ref.dtype == jnp.int16:
        value = encode(total)
    else:
        value = stacked_rows(total, out_ref.shape[1]).astype(out_ref.dtype)
    for i in range(out_ref.shape[0]):
        out_ref[i] = value


def message_of(count, values):
    return jax.ShapeDtypeStruct((count, TILE, values // TILE + LANES), jnp.int16)


def packed(parts, count):
    out = message_of(count, parts[0].size // count)
    return whole_call(encode_kernel, parts, out, "encode")


def merged(message, count, rows, width):
    out = jax.ShapeDtypeStruct((count, rows, width), jnp.bfloat16)
    return whole_call(merge_kernel, [message], out, "merge")


def merged_again(message, count):
    out = jax.ShapeDtypeStruct((count,) + message.shape[1:], jnp.int16)
    return whole_call(merge_kernel, [message], out, "merge")


def whole_call(kernel, operands, out, name, scalars=()):
    vmem = pl.BlockSpec(memory_space=pltpu.VMEM)
    smem = pl.BlockSpec(memory_space=pltpu.SMEM)
    return pl.pallas_call(
        kernel,
        in_specs=[smem] * len(scalars) + [vmem] * len(operands),
        out_specs=vmem,
        out_shape=out,
        compiler_params=pltpu.CompilerParams(vmem_limit_bytes=VMEM_LIMIT),
        name=name,
    )(*scalars, *operands)


def body(front, pattern, sample, sketch, level_ranks):
    rows, width = front.shape
    leaf_rows = rows // 2
    samples = sample.shape[0]
    half = samples // 2
    top = sketch.shape[2]
    n_leaf = lax.axis_size("leaf")
    n_samp = lax.axis_size("samp")
    depth = n_leaf.bit_length() - 1
    z = lax.axis_index("leaf")
    s = lax.axis_index("samp")
    c = lax.axis_index("cblk")
    f32 = jnp.float32
    bf16 = jnp.bfloat16

    block = 2 * s + c
    flags = lax.dynamic_slice(pattern, (2 * z, block), (2, 1))
    leaf_mask = jnp.repeat(flags, leaf_rows, axis=0).reshape(1, rows)

    def first_half(which):
        part = lax.dynamic_slice_in_dim(sample, which * half, half, 0)
        part = lax.dot_general(part, front, COLS, preferred_element_type=f32)
        return part * leaf_mask.astype(f32)

    away = swap_cores(first_half(1 - c))
    message = packed([first_half(c), away], n_samp)
    pieces = merged(exchange(message, "samp"), n_samp, half // n_samp, rows)
    mine = exchange(pieces, "samp").reshape(half, rows)
    other = swap_cores(mine)
    first_sample = jnp.where(
        c == 0, jnp.concatenate([mine, other], 0), jnp.concatenate([other, mine], 0)
    )
    first_sample = first_sample * leaf_mask.astype(bf16)

    back_part = jnp.dot(first_sample, front, preferred_element_type=f32)
    parity = (z % 2).astype(jnp.int32).reshape(1)
    pairs = []
    for i in range(n_leaf):
        pairs.append((2 * i, 2 * (i ^ 1)))
        pairs.append((2 * i + 1, 2 * ((i + 1 if i % 2 else i - 1) % n_leaf) + 1))
    group = n_leaf // 2
    form = message_of(group, samples // n_leaf * width)
    given = whole_call(give_kernel, [back_part], form, "give", [parity])
    given = lax.ppermute(given, ("leaf", "cblk"), pairs)
    message = whole_call(keep_kernel, [back_part, given], form, "keep", [parity])
    same = [list(range(p, n_leaf, 2)) for p in range(2)]
    pieces = merged(exchange(message, "leaf", same), n_leaf, samples // n_leaf, width)
    back_sample = exchange(pieces, "leaf").reshape(samples, width)

    def third_half(which):
        part = lax.dynamic_slice_in_dim(front, which * leaf_rows, leaf_rows, 0)
        flag = lax.dynamic_slice_in_dim(flags, which, 1, 0).astype(f32)
        return lax.dot_general(back_sample, part, COLS, preferred_element_type=f32) * flag

    away = swap_cores(third_half(1 - c))
    message = packed([third_half(c), away], n_samp)
    columns = exchange(merged_again(exchange(message, "samp"), n_samp), "samp")

    uppers = [c, c] + [z // 2**bit % 2 for bit in range(depth - 1)]
    table = jnp.stack([level_ranks[: len(uppers)], jnp.stack(uppers).astype(jnp.int32)], axis=1)
    leaf_basis, reduced, message = compress(0, table, [columns], sketch[0])
    path = []
    partner = swap_cores(message)
    for level in range(1, depth + 1):
        last = level == depth
        node_basis, reduced, *message = compress(
            level, table, [reduced, partner], sketch[level], last
        )
        path.append(node_basis)
        if not last:
            pairs = [(i, i ^ (1 << (level - 1))) for i in range(n_leaf)]
            partner = lax.ppermute(message[0], "leaf", pairs)
    share = samples // n_samp
    mine = lax.dynamic_slice_in_dim(reduced, s * share, share, 0)
    bit = depth - 1
    other = lax.ppermute(mine, "leaf", [(i, i ^ (1 << bit)) for i in range(n_leaf)])
    upper = z // 2**bit % 2 == 1
    root = jnp.concatenate([jnp.where(upper, other, mine), jnp.where(upper, mine, other)], axis=1)
    empty = jnp.zeros((top, 2 * top), f32)
    path = path + [empty] * (sketch.shape[0] - 1 - len(path))
    return (leaf_basis, jnp.stack(path)[None], root)


def solution(mesh):
    placed = (P("leaf", ("samp", "cblk")), P(), P(None, ("samp", "cblk")), P(), P())
    return jax.shard_map(
        body,
        mesh=mesh,
        in_specs=placed,
        out_specs=(P(None, ("leaf", "cblk")), P("leaf", None, None, None), P("samp", None)),
        check_vma=False,
    )
```

```python
import functools

import jax
import jax.numpy as jnp
from jax import lax
from jax.experimental import pallas as pl
from jax.experimental.pallas import tpu as pltpu
from jax.sharding import PartitionSpec as P

HIGHEST = lax.Precision.HIGHEST
COLS = (((1,), (1,)), ((), ()))
ROWS = (((0,), (0,)), ((), ()))
ROW_BLOCK = 16
LANES = 128
FOLD = 8
TILE = 8
VMEM_LIMIT = 16 << 20


def exact_dot(a, b, dims):
    return lax.dot_general(a, b, dims, precision=HIGHEST, preferred_element_type=jnp.float32)


def inverse_factor(gram):
    n = gram.shape[0]
    count = n // ROW_BLOCK
    lane = lax.broadcasted_iota(jnp.int32, (ROW_BLOCK, n), 1)
    row = lax.broadcasted_iota(jnp.int32, (ROW_BLOCK, n), 0)
    panels = [gram[ROW_BLOCK * i : ROW_BLOCK * (i + 1), :] for i in range(count)]
    finished = []
    for b in range(count):
        panel = panels[b]
        start = ROW_BLOCK * b
        stop = start + ROW_BLOCK
        columns = [
            jnp.broadcast_to(panel[:, start + j : start + j + 1], (ROW_BLOCK, n))
            for j in range(ROW_BLOCK)
        ]
        root = jnp.zeros((ROW_BLOCK, n), jnp.float32)
        inverse = jnp.zeros((ROW_BLOCK, n), jnp.float32)
        for k in range(ROW_BLOCK):
            pivot = jnp.broadcast_to(columns[k][k : k + 1, :], (ROW_BLOCK, n))
            over = 1.0 / pivot
            factor = jnp.where(row > k, columns[k] * over, 0.0)
            here = lane == start + k
            pivot_row = jnp.where(here, 1.0, jnp.broadcast_to(panel[k : k + 1, :], (ROW_BLOCK, n)))
            panel = jnp.where(here & (row >= k), jnp.where(row == k, 1.0, 0.0), panel)
            panel = panel - factor * pivot_row
            for j in range(k + 1, ROW_BLOCK):
                columns[j] = columns[j] - factor * jnp.broadcast_to(
                    columns[j][k : k + 1, :], (ROW_BLOCK, n)
                )
            inverse = jnp.where(row == k, over, inverse)
            root = jnp.where(row == k, lax.rsqrt(pivot), root)
        panel = jnp.where((lane <= start + row) | (lane >= stop), panel, 0.0)
        finished.append(panel * jnp.where(lane < stop, root, 0.0))
        if b + 1 < count:
            scaled = panel * inverse
            outside = (lane < start) | (lane >= stop)
            update = exact_dot(scaled[:, stop:], panel, ROWS)
            for i in range(b + 1, count):
                at = ROW_BLOCK * (i - b - 1)
                panels[i] = jnp.where(outside, panels[i], 0.0) - update[at : at + ROW_BLOCK, :]
    return jnp.concatenate(finished, axis=0)


def compress_values(parts, weights, rank):
    top = weights.shape[1]
    keep = (lax.broadcasted_iota(jnp.int32, (top, 1), 0) < rank).astype(jnp.float32)
    views = [exact_dot(weights, part, ROWS) * keep for part in parts]
    gram = sum(exact_dot(view, view, COLS) for view in views)
    at_row = lax.broadcasted_iota(jnp.int32, (top, top), 0)
    at_col = lax.broadcasted_iota(jnp.int32, (top, top), 1)
    gram = gram + jnp.where((at_row == at_col) & (at_row >= rank), 1.0, 0.0)
    cross = sum(exact_dot(part, view, COLS) for part, view in zip(parts, views, strict=True))
    inverse = inverse_factor(gram)
    bases = [exact_dot(inverse, view, (((1,), (0,)), ((), ()))) for view in views]
    return bases, exact_dot(cross, inverse, COLS)


def fold(x):
    rows = x.shape[0] // FOLD
    return jnp.concatenate([x[i * rows : (i + 1) * rows, :] for i in range(FOLD)], axis=1)


def unfold(x):
    width = x.shape[1] // FOLD
    return jnp.concatenate([x[:, i * width : (i + 1) * width] for i in range(FOLD)], axis=0)


def leaf_kernel(level, table_ref, columns_ref, weights_ref, basis_ref, reduced_ref, message_ref):
    rank = table_ref[level, 0]
    share = weights_ref.shape[0] // columns_ref.shape[0]
    columns = jnp.concatenate(
        [stacked_rows(decode(columns_ref[i]), share) for i in range(columns_ref.shape[0])], axis=0
    )
    bases, reduced = compress_values([columns], weights_ref[...], rank)
    basis_ref[...] = bases[0]
    reduced_ref[...] = reduced
    message_ref[...] = encode(fold(reduced))


def node_kernel(
    level, table_ref, mine_ref, other_ref, weights_ref, basis_ref, reduced_ref, message_ref=None
):
    upper = table_ref[level, 1] == 1
    mine = mine_ref[...]
    other = unfold(decode(other_ref[...]))
    parts = [jnp.where(upper, other, mine), jnp.where(upper, mine, other)]
    bases, reduced = compress_values(parts, weights_ref[...], table_ref[level, 0])
    top = weights_ref.shape[1]
    basis_ref[:, :top] = bases[0]
    basis_ref[:, top:] = bases[1]
    reduced_ref[...] = reduced
    if message_ref is not None:
        message_ref[...] = encode(fold(reduced))


def compress(level, table, parts, weights, last=False):
    samples, top = weights.shape
    width = (parts[0].shape[-1] - LANES) * parts[0].shape[0] * TILE // samples if len(parts) == 1 else 2 * top
    kernel = leaf_kernel if len(parts) == 1 else node_kernel
    vmem = pl.BlockSpec(memory_space=pltpu.VMEM)
    outs = [
        jax.ShapeDtypeStruct((top, width), jnp.float32),
        jax.ShapeDtypeStruct((samples, top), jnp.float32),
        jax.ShapeDtypeStruct((samples // FOLD, FOLD * top + LANES), jnp.int16),
    ]
    outs = outs[:2] if last else outs
    return pl.pallas_call(
        functools.partial(kernel, level),
        in_specs=[pl.BlockSpec(memory_space=pltpu.SMEM)] + [vmem] * (len(parts) + 1),
        out_specs=(vmem,) * len(outs),
        out_shape=tuple(outs),
        compiler_params=pltpu.CompilerParams(vmem_limit_bytes=VMEM_LIMIT),
        name="compress_leaf" if len(parts) == 1 else "compress_node",
    )(table, *parts, weights)


def swap_cores(x):
    return lax.ppermute(x, "cblk", [(0, 1), (1, 0)])


def exchange(x, axis, groups=None):
    return lax.all_to_all(x, axis, 0, 0, axis_index_groups=groups)


def encode(x):
    lane = lax.broadcasted_iota(jnp.int32, (x.shape[0], LANES), 1)
    tail = jnp.zeros((x.shape[0], LANES), jnp.float32)
    tiles = []
    for g in range(x.shape[1] // LANES):
        tile = x[:, g * LANES : (g + 1) * LANES]
        top = jnp.max(jnp.abs(tile), axis=1, keepdims=True)
        bits = jnp.clip(15.0 - jnp.ceil(jnp.log2(top * 1.001)), -120.0, 120.0)
        bits = jnp.broadcast_to(jnp.where(top > 0, bits, 0.0), tile.shape)
        tiles.append(jnp.round(tile * jnp.exp2(bits)))
        tail = jnp.where(lane == g, bits, tail)
    return jnp.concatenate(tiles + [tail], axis=1).astype(jnp.int32).astype(jnp.int16)


def decode(message):
    wide = message.astype(jnp.int32).astype(jnp.float32)
    width = wide.shape[1] - LANES
    scale = jnp.exp2(-wide[:, width:])
    return jnp.concatenate(
        [
            wide[:, g * LANES : (g + 1) * LANES] * scale[:, g : g + 1]
            for g in range(width // LANES)
        ],
        axis=1,
    )


def side_by_side(x):
    return jnp.concatenate([x[:TILE, :], x[TILE:, :]], axis=1) if x.shape[0] > TILE else x


def stacked_rows(x, rows):
    if rows == TILE:
        return x
    width = x.shape[1] // 2
    return jnp.concatenate([x[:, :width], x[:, width:]], axis=0)


def encode_kernel(*refs):
    out_ref = refs[-1]
    count = out_ref.shape[0]
    rows = refs[0].shape[0] // count
    for i in range(count):
        at = pl.ds(i * rows, rows)
        out_ref[i] = encode(side_by_side(sum(ref[at, :] for ref in refs[:-1])))


def give_kernel(parity_ref, part_ref, out_ref):
    count = out_ref.shape[0]
    rows = part_ref.shape[0] // (2 * count)
    other = 1 - parity_ref[0]
    for i in range(count):
        at = pl.multiple_of((2 * i + other) * rows, rows)
        out_ref[i] = encode(side_by_side(part_ref[pl.ds(at, rows), :]))


def keep_kernel(parity_ref, part_ref, message_ref, out_ref):
    count = out_ref.shape[0]
    rows = part_ref.shape[0] // (2 * count)
    for i in range(count):
        at = pl.multiple_of((2 * i + parity_ref[0]) * rows, rows)
        kept = side_by_side(part_ref[pl.ds(at, rows), :])
        out_ref[i] = encode(kept + decode(message_ref[i]))


def merge_kernel(message_ref, out_ref):
    total = decode(message_ref[0])
    for i in range(1, message_ref.shape[0]):
        total = total + decode(message_ref[i])
    if out_ref.dtype == jnp.int16:
        value = encode(total)
    else:
        value = stacked_rows(total, out_ref.shape[1]).astype(out_ref.dtype)
    for i in range(out_ref.shape[0]):
        out_ref[i] = value


def message_of(count, values):
    return jax.ShapeDtypeStruct((count, TILE, values // TILE + LANES), jnp.int16)


def packed(parts, count):
    out = message_of(count, parts[0].size // count)
    return whole_call(encode_kernel, parts, out, "encode")


def merged(message, count, rows, width):
    out = jax.ShapeDtypeStruct((count, rows, width), jnp.bfloat16)
    return whole_call(merge_kernel, [message], out, "merge")


def merged_again(message, count):
    out = jax.ShapeDtypeStruct((count,) + message.shape[1:], jnp.int16)
    return whole_call(merge_kernel, [message], out, "merge")


def whole_call(kernel, operands, out, name, scalars=()):
    vmem = pl.BlockSpec(memory_space=pltpu.VMEM)
    smem = pl.BlockSpec(memory_space=pltpu.SMEM)
    return pl.pallas_call(
        kernel,
        in_specs=[smem] * len(scalars) + [vmem] * len(operands),
        out_specs=vmem,
        out_shape=out,
        compiler_params=pltpu.CompilerParams(vmem_limit_bytes=VMEM_LIMIT),
        name=name,
    )(*scalars, *operands)


def body(front, pattern, sample, sketch, level_ranks):
    rows, width = front.shape
    leaf_rows = rows // 2
    samples = sample.shape[0]
    top = sketch.shape[2]
    n_leaf = lax.axis_size("leaf")
    n_samp = lax.axis_size("samp")
    depth = n_leaf.bit_length() - 1
    z = lax.axis_index("leaf")
    s = lax.axis_index("samp")
    c = lax.axis_index("cblk")
    f32 = jnp.float32
    bf16 = jnp.bfloat16

    block = 2 * s + c
    flags = lax.dynamic_slice(pattern, (2 * z, block), (2, 1)).astype(f32)

    def of_leaf(which):
        part = lax.dynamic_slice_in_dim(front, which * leaf_rows, leaf_rows, 0)
        return part, lax.dynamic_slice_in_dim(flags, which, 1, 0)

    def onto_leaf(which, left):
        part, flag = of_leaf(which)
        return lax.dot_general(left, part, COLS, preferred_element_type=f32) * flag

    def from_leaf(which, left):
        part, flag = of_leaf(which)
        return jnp.dot(left, part, preferred_element_type=f32) * flag

    away = swap_cores(onto_leaf(1 - c, sample))
    message = packed([onto_leaf(c, sample), away], n_samp)
    share = samples // n_samp
    pieces = merged(exchange(message, "samp"), n_samp, share, leaf_rows)
    mine = exchange(pieces, "samp").reshape(samples, leaf_rows)
    other = swap_cores(mine)

    back_part = lax.optimization_barrier(from_leaf(c, mine)) + from_leaf(1 - c, other)
    parity = (z % 2).astype(jnp.int32).reshape(1)
    pairs = []
    for i in range(n_leaf):
        pairs.append((2 * i, 2 * (i ^ 1)))
        pairs.append((2 * i + 1, 2 * ((i + 1 if i % 2 else i - 1) % n_leaf) + 1))
    group = n_leaf // 2
    form = message_of(group, samples // n_leaf * width)
    given = whole_call(give_kernel, [back_part], form, "give", [parity])
    given = lax.ppermute(given, ("leaf", "cblk"), pairs)
    message = whole_call(keep_kernel, [back_part, given], form, "keep", [parity])
    same = [list(range(p, n_leaf, 2)) for p in range(2)]
    pieces = merged(exchange(message, "leaf", same), n_leaf, samples // n_leaf, width)
    back_sample = exchange(pieces, "leaf").reshape(samples, width)

    away = swap_cores(onto_leaf(1 - c, back_sample))
    message = packed([onto_leaf(c, back_sample), away], n_samp)
    columns = exchange(merged_again(exchange(message, "samp"), n_samp), "samp")

    uppers = [c, c] + [z // 2**bit % 2 for bit in range(depth - 1)]
    table = jnp.stack([level_ranks[: len(uppers)], jnp.stack(uppers).astype(jnp.int32)], axis=1)
    leaf_basis, reduced, message = compress(0, table, [columns], sketch[0])
    path = []
    partner = swap_cores(message)
    for level in range(1, depth + 1):
        last = level == depth
        node_basis, reduced, *message = compress(
            level, table, [reduced, partner], sketch[level], last
        )
        path.append(node_basis)
        if not last:
            pairs = [(i, i ^ (1 << (level - 1))) for i in range(n_leaf)]
            partner = lax.ppermute(message[0], "leaf", pairs)
    mine = lax.dynamic_slice_in_dim(reduced, s * share, share, 0)
    bit = depth - 1
    other = lax.ppermute(mine, "leaf", [(i, i ^ (1 << bit)) for i in range(n_leaf)])
    upper = z // 2**bit % 2 == 1
    root = jnp.concatenate([jnp.where(upper, other, mine), jnp.where(upper, mine, other)], axis=1)
    empty = jnp.zeros((top, 2 * top), f32)
    path = path + [empty] * (sketch.shape[0] - 1 - len(path))
    return (leaf_basis, jnp.stack(path)[None], root)


def solution(mesh):
    placed = (P("leaf", ("samp", "cblk")), P(), P(None, ("samp", "cblk")), P(), P())
    return jax.shard_map(
        body,
        mesh=mesh,
        in_specs=placed,
        out_specs=(P(None, ("leaf", "cblk")), P("leaf", None, None, None), P("samp", None)),
        check_vma=False,
    )
```

```python
import functools

import jax
import jax.numpy as jnp
from jax import lax
from jax.experimental import pallas as pl
from jax.experimental.pallas import tpu as pltpu
from jax.sharding import PartitionSpec as P

HIGHEST = lax.Precision.HIGHEST
COLS = (((1,), (1,)), ((), ()))
ROWS = (((0,), (0,)), ((), ()))
ROW_BLOCK = 16
LANES = 128
FOLD = 8
TILE = 8
VMEM_LIMIT = 16 << 20


def exact_dot(a, b, dims):
    return lax.dot_general(a, b, dims, precision=HIGHEST, preferred_element_type=jnp.float32)


def inverse_factor(gram):
    n = gram.shape[0]
    count = n // ROW_BLOCK
    lane = lax.broadcasted_iota(jnp.int32, (ROW_BLOCK, n), 1)
    row = lax.broadcasted_iota(jnp.int32, (ROW_BLOCK, n), 0)
    panels = [gram[ROW_BLOCK * i : ROW_BLOCK * (i + 1), :] for i in range(count)]
    finished = []
    for b in range(count):
        panel = panels[b]
        start = ROW_BLOCK * b
        stop = start + ROW_BLOCK
        columns = [
            jnp.broadcast_to(panel[:, start + j : start + j + 1], (ROW_BLOCK, n))
            for j in range(ROW_BLOCK)
        ]
        root = jnp.zeros((ROW_BLOCK, n), jnp.float32)
        inverse = jnp.zeros((ROW_BLOCK, n), jnp.float32)
        for k in range(ROW_BLOCK):
            pivot = jnp.broadcast_to(columns[k][k : k + 1, :], (ROW_BLOCK, n))
            over = 1.0 / pivot
            factor = jnp.where(row > k, columns[k] * over, 0.0)
            here = lane == start + k
            pivot_row = jnp.where(here, 1.0, jnp.broadcast_to(panel[k : k + 1, :], (ROW_BLOCK, n)))
            panel = jnp.where(here & (row >= k), jnp.where(row == k, 1.0, 0.0), panel)
            panel = panel - factor * pivot_row
            for j in range(k + 1, ROW_BLOCK):
                columns[j] = columns[j] - factor * jnp.broadcast_to(
                    columns[j][k : k + 1, :], (ROW_BLOCK, n)
                )
            inverse = jnp.where(row == k, over, inverse)
            root = jnp.where(row == k, lax.rsqrt(pivot), root)
        panel = jnp.where((lane <= start + row) | (lane >= stop), panel, 0.0)
        finished.append(panel * jnp.where(lane < stop, root, 0.0))
        if b + 1 < count:
            scaled = panel * inverse
            outside = (lane < start) | (lane >= stop)
            column = jnp.transpose(scaled)[stop : stop + ROW_BLOCK, :]
            terms = [
                jnp.broadcast_to(column[:, k : k + 1], (ROW_BLOCK, n))
                * jnp.broadcast_to(panel[k : k + 1, :], (ROW_BLOCK, n))
                for k in range(ROW_BLOCK)
            ]
            while len(terms) > 1:
                terms = [terms[i] + terms[i + 1] for i in range(0, len(terms), 2)]
            panels[b + 1] = jnp.where(outside, panels[b + 1], 0.0) - terms[0]
            if b + 2 < count:
                update = exact_dot(scaled[:, stop + ROW_BLOCK :], panel, ROWS)
                for i in range(b + 2, count):
                    at = ROW_BLOCK * (i - b - 2)
                    panels[i] = jnp.where(outside, panels[i], 0.0) - update[at : at + ROW_BLOCK, :]
    return jnp.concatenate(finished, axis=0)


def compress_values(parts, weights, rank):
    top = weights.shape[1]
    keep = (lax.broadcasted_iota(jnp.int32, (top, 1), 0) < rank).astype(jnp.float32)
    views = [exact_dot(weights, part, ROWS) * keep for part in parts]
    gram = sum(exact_dot(view, view, COLS) for view in views)
    at_row = lax.broadcasted_iota(jnp.int32, (top, top), 0)
    at_col = lax.broadcasted_iota(jnp.int32, (top, top), 1)
    gram = gram + jnp.where((at_row == at_col) & (at_row >= rank), 1.0, 0.0)
    cross = sum(exact_dot(part, view, COLS) for part, view in zip(parts, views, strict=True))
    inverse = inverse_factor(gram)
    bases = [exact_dot(inverse, view, (((1,), (0,)), ((), ()))) for view in views]
    return bases, exact_dot(cross, inverse, COLS)


def fold(x):
    rows = x.shape[0] // FOLD
    return jnp.concatenate([x[i * rows : (i + 1) * rows, :] for i in range(FOLD)], axis=1)


def unfold(x):
    width = x.shape[1] // FOLD
    return jnp.concatenate([x[:, i * width : (i + 1) * width] for i in range(FOLD)], axis=0)


def leaf_kernel(level, table_ref, columns_ref, weights_ref, basis_ref, reduced_ref, message_ref):
    rank = table_ref[level, 0]
    share = weights_ref.shape[0] // columns_ref.shape[0]
    columns = jnp.concatenate(
        [stacked_rows(decode(columns_ref[i]), share) for i in range(columns_ref.shape[0])], axis=0
    )
    bases, reduced = compress_values([columns], weights_ref[...], rank)
    basis_ref[...] = bases[0]
    reduced_ref[...] = reduced
    message_ref[...] = encode(fold(reduced))


def node_kernel(
    level, table_ref, mine_ref, other_ref, weights_ref, basis_ref, reduced_ref, message_ref=None
):
    upper = table_ref[level, 1] == 1
    mine = mine_ref[...]
    other = unfold(decode(other_ref[...]))
    parts = [jnp.where(upper, other, mine), jnp.where(upper, mine, other)]
    bases, reduced = compress_values(parts, weights_ref[...], table_ref[level, 0])
    top = weights_ref.shape[1]
    basis_ref[:, :top] = bases[0]
    basis_ref[:, top:] = bases[1]
    reduced_ref[...] = reduced
    if message_ref is not None:
        message_ref[...] = encode(fold(reduced))


def compress(level, table, parts, weights, last=False):
    samples, top = weights.shape
    width = (parts[0].shape[-1] - LANES) * parts[0].shape[0] * TILE // samples if len(parts) == 1 else 2 * top
    kernel = leaf_kernel if len(parts) == 1 else node_kernel
    vmem = pl.BlockSpec(memory_space=pltpu.VMEM)
    outs = [
        jax.ShapeDtypeStruct((top, width), jnp.float32),
        jax.ShapeDtypeStruct((samples, top), jnp.float32),
        jax.ShapeDtypeStruct((samples // FOLD, FOLD * top + LANES), jnp.int16),
    ]
    outs = outs[:2] if last else outs
    return pl.pallas_call(
        functools.partial(kernel, level),
        in_specs=[pl.BlockSpec(memory_space=pltpu.SMEM)] + [vmem] * (len(parts) + 1),
        out_specs=(vmem,) * len(outs),
        out_shape=tuple(outs),
        compiler_params=pltpu.CompilerParams(vmem_limit_bytes=VMEM_LIMIT),
        name="compress_leaf" if len(parts) == 1 else "compress_node",
    )(table, *parts, weights)


def swap_cores(x):
    return lax.ppermute(x, "cblk", [(0, 1), (1, 0)])


def exchange(x, axis, groups=None):
    return lax.all_to_all(x, axis, 0, 0, axis_index_groups=groups)


def encode(x):
    lane = lax.broadcasted_iota(jnp.int32, (x.shape[0], LANES), 1)
    tail = jnp.zeros((x.shape[0], LANES), jnp.float32)
    tiles = []
    for g in range(x.shape[1] // LANES):
        tile = x[:, g * LANES : (g + 1) * LANES]
        top = jnp.max(jnp.abs(tile), axis=1, keepdims=True)
        bits = jnp.clip(15.0 - jnp.ceil(jnp.log2(top * 1.001)), -120.0, 120.0)
        bits = jnp.broadcast_to(jnp.where(top > 0, bits, 0.0), tile.shape)
        tiles.append(jnp.round(tile * jnp.exp2(bits)))
        tail = jnp.where(lane == g, bits, tail)
    return jnp.concatenate(tiles + [tail], axis=1).astype(jnp.int32).astype(jnp.int16)


def decode(message):
    wide = message.astype(jnp.int32).astype(jnp.float32)
    width = wide.shape[1] - LANES
    scale = jnp.exp2(-wide[:, width:])
    return jnp.concatenate(
        [
            wide[:, g * LANES : (g + 1) * LANES] * scale[:, g : g + 1]
            for g in range(width // LANES)
        ],
        axis=1,
    )


def side_by_side(x):
    return jnp.concatenate([x[:TILE, :], x[TILE:, :]], axis=1) if x.shape[0] > TILE else x


def stacked_rows(x, rows):
    if rows == TILE:
        return x
    width = x.shape[1] // 2
    return jnp.concatenate([x[:, :width], x[:, width:]], axis=0)


def encode_kernel(*refs):
    out_ref = refs[-1]
    count = out_ref.shape[0]
    rows = refs[0].shape[0] // count
    for i in range(count):
        at = pl.ds(i * rows, rows)
        out_ref[i] = encode(side_by_side(sum(ref[at, :] for ref in refs[:-1])))


def give_kernel(parity_ref, part_ref, out_ref):
    count = out_ref.shape[0]
    rows = part_ref.shape[0] // (2 * count)
    other = 1 - parity_ref[0]
    for i in range(count):
        at = pl.multiple_of((2 * i + other) * rows, rows)
        out_ref[i] = encode(side_by_side(part_ref[pl.ds(at, rows), :]))


def keep_kernel(parity_ref, part_ref, message_ref, out_ref):
    count = out_ref.shape[0]
    rows = part_ref.shape[0] // (2 * count)
    for i in range(count):
        at = pl.multiple_of((2 * i + parity_ref[0]) * rows, rows)
        kept = side_by_side(part_ref[pl.ds(at, rows), :])
        out_ref[i] = encode(kept + decode(message_ref[i]))


def merge_kernel(message_ref, out_ref):
    total = decode(message_ref[0])
    for i in range(1, message_ref.shape[0]):
        total = total + decode(message_ref[i])
    if out_ref.dtype == jnp.int16:
        value = encode(total)
    else:
        value = stacked_rows(total, out_ref.shape[1]).astype(out_ref.dtype)
    for i in range(out_ref.shape[0]):
        out_ref[i] = value


def message_of(count, values):
    return jax.ShapeDtypeStruct((count, TILE, values // TILE + LANES), jnp.int16)


def packed(parts, count):
    out = message_of(count, parts[0].size // count)
    return whole_call(encode_kernel, parts, out, "encode")


def merged(message, count, rows, width):
    out = jax.ShapeDtypeStruct((count, rows, width), jnp.bfloat16)
    return whole_call(merge_kernel, [message], out, "merge")


def merged_again(message, count):
    out = jax.ShapeDtypeStruct((count,) + message.shape[1:], jnp.int16)
    return whole_call(merge_kernel, [message], out, "merge")


def whole_call(kernel, operands, out, name, scalars=()):
    vmem = pl.BlockSpec(memory_space=pltpu.VMEM)
    smem = pl.BlockSpec(memory_space=pltpu.SMEM)
    return pl.pallas_call(
        kernel,
        in_specs=[smem] * len(scalars) + [vmem] * len(operands),
        out_specs=vmem,
        out_shape=out,
        compiler_params=pltpu.CompilerParams(vmem_limit_bytes=VMEM_LIMIT),
        name=name,
    )(*scalars, *operands)


def body(front, pattern, sample, sketch, level_ranks):
    rows, width = front.shape
    leaf_rows = rows // 2
    samples = sample.shape[0]
    top = sketch.shape[2]
    n_leaf = lax.axis_size("leaf")
    n_samp = lax.axis_size("samp")
    depth = n_leaf.bit_length() - 1
    z = lax.axis_index("leaf")
    s = lax.axis_index("samp")
    c = lax.axis_index("cblk")
    f32 = jnp.float32
    bf16 = jnp.bfloat16

    block = 2 * s + c
    flags = lax.dynamic_slice(pattern, (2 * z, block), (2, 1)).astype(f32)

    def of_leaf(which):
        part = lax.dynamic_slice_in_dim(front, which * leaf_rows, leaf_rows, 0)
        return part, lax.dynamic_slice_in_dim(flags, which, 1, 0)

    def onto_leaf(which, left):
        part, flag = of_leaf(which)
        return lax.dot_general(left, part, COLS, preferred_element_type=f32) * flag

    def from_leaf(which, left):
        part, flag = of_leaf(which)
        return jnp.dot(left, part, preferred_element_type=f32) * flag

    away = swap_cores(onto_leaf(1 - c, sample))
    message = packed([onto_leaf(c, sample), away], n_samp)
    share = samples // n_samp
    pieces = merged(exchange(message, "samp"), n_samp, share, leaf_rows)
    mine = exchange(pieces, "samp").reshape(samples, leaf_rows)
    other = swap_cores(mine)

    back_part = lax.optimization_barrier(from_leaf(c, mine)) + from_leaf(1 - c, other)
    parity = (z % 2).astype(jnp.int32).reshape(1)
    pairs = []
    for i in range(n_leaf):
        pairs.append((2 * i, 2 * (i ^ 1)))
        pairs.append((2 * i + 1, 2 * ((i + 1 if i % 2 else i - 1) % n_leaf) + 1))
    group = n_leaf // 2
    form = message_of(group, samples // n_leaf * width)
    given = whole_call(give_kernel, [back_part], form, "give", [parity])
    given = lax.ppermute(given, ("leaf", "cblk"), pairs)
    message = whole_call(keep_kernel, [back_part, given], form, "keep", [parity])
    same = [list(range(p, n_leaf, 2)) for p in range(2)]
    pieces = merged(exchange(message, "leaf", same), n_leaf, samples // n_leaf, width)
    back_sample = exchange(pieces, "leaf").reshape(samples, width)

    away = swap_cores(onto_leaf(1 - c, back_sample))
    message = packed([onto_leaf(c, back_sample), away], n_samp)
    columns = exchange(merged_again(exchange(message, "samp"), n_samp), "samp")

    uppers = [c, c] + [z // 2**bit % 2 for bit in range(depth - 1)]
    table = jnp.stack([level_ranks[: len(uppers)], jnp.stack(uppers).astype(jnp.int32)], axis=1)
    leaf_basis, reduced, message = compress(0, table, [columns], sketch[0])
    path = []
    partner = swap_cores(message)
    for level in range(1, depth + 1):
        last = level == depth
        node_basis, reduced, *message = compress(
            level, table, [reduced, partner], sketch[level], last
        )
        path.append(node_basis)
        if not last:
            pairs = [(i, i ^ (1 << (level - 1))) for i in range(n_leaf)]
            partner = lax.ppermute(message[0], "leaf", pairs)
    mine = lax.dynamic_slice_in_dim(reduced, s * share, share, 0)
    bit = depth - 1
    other = lax.ppermute(mine, "leaf", [(i, n_leaf - 1 - i) for i in range(n_leaf)])
    upper = z // 2**bit % 2 == 1
    root = jnp.concatenate([jnp.where(upper, other, mine), jnp.where(upper, mine, other)], axis=1)
    empty = jnp.zeros((top, 2 * top), f32)
    path = path + [empty] * (sketch.shape[0] - 1 - len(path))
    return (leaf_basis, jnp.stack(path)[None], root)


def solution(mesh):
    placed = (P("leaf", ("samp", "cblk")), P(), P(None, ("samp", "cblk")), P(), P())
    return jax.shard_map(
        body,
        mesh=mesh,
        in_specs=placed,
        out_specs=(P(None, ("leaf", "cblk")), P("leaf", None, None, None), P("samp", None)),
        check_vma=False,
    )
```
